32 devices in a mesh: pipe: 2 (over core), seq: 4 (over z), dp: 4 (over y, x).
Axes of the slice: x: 2, y: 2, z: 4, core: 2. Of those that a mesh axis runs over, the one named last changes fastest.
Arguments:
- images: bfloat16 [8, 1376, 1024], P('dp', 'seq'), may hold values from -6 to 6
- key_mask: int32 [8, 1376], P('dp', 'seq'), may hold values from 0 to 1, as said below
- w_qkv: bfloat16 [2, 1024, 3072], P('pipe', 'dp'), may hold values from -0.1875 to 0.1875
- w_proj: bfloat16 [2, 1024, 1024], P('pipe', 'dp'), may hold values from -0.375 to 0.375
- w_fc1: bfloat16 [2, 1024, 4096], P('pipe', 'dp'), may hold values from -0.1875 to 0.1875
- w_fc2: bfloat16 [2, 4096, 1024], P('pipe', 'dp'), may hold values from -0.09375 to 0.09375
- gains: float32 [2, 4, 1024], P('pipe', None, 'dp'), may hold values from 0.1 to 1.9
- biases: float32 [2, 6, 1024], P('pipe', None, 'dp'), may hold values from -1.8 to 1.8
- fc1_bias: float32 [2, 4096], P('pipe', 'dp'), may hold values from -1.8 to 1.8
- out_grad: bfloat16 [8, 1376, 1024], P('dp', 'seq'), may hold values from -6 to 6
Outputs:
- section_outputs: bfloat16 [2, 8, 1376, 1024], P('pipe', 'dp', 'seq')
- input_grads: bfloat16 [2, 8, 1376, 1024], P('pipe', 'dp', 'seq')
- grad_qkv: float32 [2, 1024, 3072], P('pipe', ('seq', 'dp'))
- grad_proj: float32 [2, 1024, 1024], P('pipe', ('seq', 'dp'))
- grad_fc1: float32 [2, 1024, 4096], P('pipe', ('seq', 'dp'))
- grad_fc2: float32 [2, 4096, 1024], P('pipe', ('seq', 'dp'))
- grad_gains: float32 [2, 4, 1024], P('pipe', None, ('seq', 'dp'))
- grad_biases: float32 [2, 6, 1024], P('pipe', None, ('seq', 'dp'))
- grad_fc1_bias: float32 [2, 4096], P('pipe', ('seq', 'dp'))
The draws below stay inside these ranges and needn't reach their ends.
Inputs may be any that keep to these rules, and one draw needn't show every extreme that they name: In every image the ones of key_mask are a prefix of its tokens, 688 tokens long or longer.
All inputs are finite; a program needn't handle non-finite values.
Results may differ from the reference program's by a relative error of at most 0.03.
Values may be sent and summed in bfloat16 or wider, within the bound.
A program may use at most 256 MiB of HBM per device.

```python
import jax
import jax.numpy as jnp
from jax import lax

D = 1024
H = 16
HD = 64
FF = 4096
L = 1376
IMAGES = 8


def draw_key_mask(key, part):
    lengths = jax.random.randint(key, (IMAGES,), L // 2, L + 1)
    lengths = jnp.where(jnp.arange(IMAGES) == 0, L // 2, lengths)
    positions = jnp.arange(L)
    return (positions[None, :] < lengths[:, None]).astype(jnp.int32)


def block_levels(stream_key, dims, split, low, largest):
    gain, own = 1.0, jax.random.fold_in(stream_key, 6)
    for position, parts in split:
        heights = jnp.exp(jax.random.uniform(jax.random.fold_in(own, position), (parts,), jnp.float32, low / len(split), largest / len(split)))
        gain = gain * jnp.repeat(heights, dims[position] // parts).reshape([-1 if axis == position else 1 for axis in range(len(dims))])
    return gain


def scatter_about(stream_key, extent, width, bound, split=(), dtype=jnp.bfloat16):
    loudness = block_levels(stream_key, extent, split, -0.22, 0.18) if split else 1.0
    result = jax.random.normal(stream_key, extent, jnp.float32) * width * loudness
    return jnp.minimum(jnp.maximum(result, -bound), bound).astype(dtype)


def setup_inputs(seed: int = 0) -> dict:
    key_list = jax.random.split(jax.random.key(seed), 11)
    images = scatter_about(key_list[0], (IMAGES, L, D), 1.0, 6.0, ((0, 4), (1, 4)))
    key_mask = draw_key_mask(jax.random.fold_in(key_list[10], 71), 0)
    w_qkv = scatter_about(key_list[2], (2, D, 3 * D), D ** -0.5, 0.1875, ((0, 2), (1, 4)))
    w_proj = scatter_about(key_list[3], (2, D, D), (D // 4) ** -0.5, 0.375, ((0, 2), (1, 4)))
    w_fc1 = scatter_about(key_list[4], (2, D, FF), D ** -0.5, 0.1875, ((0, 2), (1, 4)))
    w_fc2 = scatter_about(key_list[5], (2, FF, D), FF ** -0.5, 0.09375, ((0, 2), (1, 4)))
    gains = jnp.clip(1.0 + 0.18 * jax.random.normal(key_list[6], (2, 4, D), jnp.float32), 0.1, 1.9)
    biases = scatter_about(key_list[7], (2, 6, D), 0.3, 1.8, ((0, 2), (2, 4)), jnp.float32)
    fc1_bias = scatter_about(key_list[8], (2, FF), 0.3, 1.8, ((0, 2), (1, 4)), jnp.float32)
    out_grad = scatter_about(key_list[9], (IMAGES, L, D), 1.0, 6.0, ((0, 4), (1, 4)))
    return dict(images=images, key_mask=key_mask, w_qkv=w_qkv, w_proj=w_proj, w_fc1=w_fc1, w_fc2=w_fc2, gains=gains, biases=biases, fc1_bias=fc1_bias, out_grad=out_grad)


epsilon = 1e-06
highest = lax.Precision.HIGHEST

@jax.custom_vjp
def low(v):
    return lax.optimization_barrier(v.astype(jnp.bfloat16)).astype(jnp.float32)

@jax.custom_vjp
def low_back(v):
    return v

def low_keep(v):
    return (low(v), None)

def low_pass(kept, grad):
    return (grad,)

def back_keep(v):
    return (v, None)

def back_low(kept, grad):
    return (low(grad),)
low.defvjp(low_keep, low_pass)
low_back.defvjp(back_keep, back_low)

def normalize(values):
    centre = lax.optimization_barrier(jnp.mean(values, axis=-1, keepdims=True))
    shifted = values - centre
    return shifted * lax.rsqrt(lax.optimization_barrier(jnp.mean(shifted * shifted, axis=-1, keepdims=True)) + epsilon)

def attend_head(pieces):
    queries, key_rows, values, visible = pieces
    scores = low_back(jnp.dot(queries, key_rows.T, precision=highest, preferred_element_type=jnp.float32) * 0.125)
    scores = jnp.where(visible[None, :], scores, -1e+30)
    attention = jax.nn.softmax(scores, axis=-1)
    return jnp.dot(low(attention), values, precision=highest, preferred_element_type=jnp.float32)

def layer_apply(inputs, visible, w_qkv, w_proj, w_fc1, w_fc2, gains, biases, fc1_bias):
    image_count = inputs.shape[0]
    normed_in = low(normalize(inputs) * gains[0] + biases[0])
    projected = jnp.einsum('bld,de->ble', normed_in, w_qkv, precision=highest)
    queries = low(low_back(projected[..., :D] + biases[1]))
    key_rows = low(low_back(projected[..., D:2 * D]))
    values = low(low_back(projected[..., 2 * D:] + biases[2]))

    def split_heads(tensor):
        return tensor.reshape(image_count, L, H, HD).transpose(0, 2, 1, 3).reshape(image_count * H, L, HD)
    visible_rows = jnp.repeat(visible, H, axis=0)
    head_outs = lax.map(jax.checkpoint(attend_head), (split_heads(queries), split_heads(key_rows), split_heads(values), visible_rows))
    merged = low(low_back(head_outs.reshape(image_count, H, L, HD).transpose(0, 2, 1, 3).reshape(image_count, L, D)))
    branch_one = low_back(jnp.einsum('bld,de->ble', merged, w_proj, precision=highest) + biases[3])
    residual = inputs + gains[1] * branch_one
    second = low(normalize(residual) * gains[2] + biases[4])
    hidden = low_back(jnp.einsum('bld,df->blf', second, w_fc1, precision=highest) + fc1_bias)
    active = low(jax.nn.gelu(hidden, approximate=False))
    branch_two = low_back(jnp.einsum('blf,fd->bld', active, w_fc2, precision=highest) + biases[5])
    return residual + gains[3] * branch_two

def reference(images, key_mask, w_qkv, w_proj, w_fc1, w_fc2, gains, biases, fc1_bias, out_grad):
    sections = []
    for section_no in range(2):
        sections.append(tuple((tensor[section_no].astype(jnp.float32) for tensor in (w_qkv, w_proj, w_fc1, w_fc2, gains, biases, fc1_bias))))
    groups = IMAGES // 2
    inputs_all = images.astype(jnp.float32).reshape(groups, 2, L, D)
    masks_all = (key_mask > 0).reshape(groups, 2, L)
    upstream_all = out_grad.astype(jnp.float32).reshape(groups, 2, L, D)
    zeros_init = tuple((tuple((jnp.zeros(tensor.shape, jnp.float32) for tensor in section)) for section in sections))

    def one_group(carry, inputs_now):
        frames, visible, upstream = inputs_now
        first_out, back_first = jax.vjp(lambda frames_in, *params: layer_apply(frames_in, visible, *params), frames, *sections[0])
        sent = first_out.astype(jnp.bfloat16)
        second_out, back_second = jax.vjp(lambda frames_in, *params: layer_apply(frames_in, visible, *params), sent.astype(jnp.float32), *sections[1])
        grads_second = back_second(upstream)
        returned = grads_second[0].astype(jnp.bfloat16)
        grads_first = back_first(returned.astype(jnp.float32))
        carry_first = tuple((previous + update for previous, update in zip(carry[0], grads_first[1:])))
        carry_second = tuple((previous + update for previous, update in zip(carry[1], grads_second[1:])))
        return ((carry_first, carry_second), (sent, second_out.astype(jnp.bfloat16), grads_first[0].astype(jnp.bfloat16), returned))
    (acc_first, acc_second), (firsts, seconds, back_ins, back_mids) = lax.scan(one_group, zeros_init, (inputs_all, masks_all, upstream_all))
    section_outputs = jnp.stack([firsts.reshape(IMAGES, L, D), seconds.reshape(IMAGES, L, D)])
    input_grads = jnp.stack([back_ins.reshape(IMAGES, L, D), back_mids.reshape(IMAGES, L, D)])
    return (section_outputs, input_grads, jnp.stack([acc_first[0], acc_second[0]]), jnp.stack([acc_first[1], acc_second[1]]), jnp.stack([acc_first[2], acc_second[2]]), jnp.stack([acc_first[3], acc_second[3]]), jnp.stack([acc_first[4], acc_second[4]]), jnp.stack([acc_first[5], acc_second[5]]), jnp.stack([acc_first[6], acc_second[6]]))
```

```python
import functools

import jax
import jax.numpy as jnp
from jax import lax
from jax.experimental import pallas as pl
from jax.experimental.pallas import tpu as pltpu
from jax.sharding import PartitionSpec as P

D = 1024
H = 16
HD = 64

epsilon = 1e-06
root_half = 0.7071067811865476
inv_root_tau = 0.3989422804014327
ALL = ("seq", "dp", "pipe")
F32 = jnp.float32
BF16 = jnp.bfloat16


def layer_norm(values):
    centre = jnp.mean(values, axis=-1, keepdims=True)
    shifted = values - centre
    factor = lax.rsqrt(jnp.mean(shifted * shifted, axis=-1, keepdims=True) + epsilon)
    return (shifted * factor, factor)


def norm_back(upward, normed, factor):
    inner = (
        upward
        - jnp.mean(upward, axis=-1, keepdims=True)
        - normed * jnp.mean(upward * normed, axis=-1, keepdims=True)
    )
    return factor * inner


def gelu_value(hidden):
    return 0.5 * hidden * (1.0 + lax.erf(hidden * root_half))


def gelu_slope(hidden):
    return (
        0.5 * (1.0 + lax.erf(hidden * root_half))
        + hidden * jnp.exp(-0.5 * hidden * hidden) * inv_root_tau
    )


def swap(block):
    return lax.ppermute(block, "pipe", [(0, 1), (1, 0)])


def to_sections(first, second, axis):
    low = lax.axis_index("pipe") == 0
    mine = jnp.where(low, first, second)
    theirs = swap(jnp.where(low, second, first))
    return jnp.where(
        low,
        jnp.concatenate([mine, theirs], axis=axis),
        jnp.concatenate([theirs, mine], axis=axis),
    )


NT = (((1,), (1,)), ((), ()))
NN = (((1,), (0,)), ((), ()))
TN = (((0,), (0,)), ((), ()))


def dot(a, b, dims):
    return lax.dot_general(a, b, dims, preferred_element_type=F32)


def forward_kernel(heads, q_ref, k_ref, v_ref, bias_ref, o_ref, lse_ref):
    bias = bias_ref[0]
    outs, sums = [], []
    for h in range(heads):
        cols = slice(h * HD, (h + 1) * HD)
        s = dot(q_ref[0, :, cols] * jnp.asarray(0.125, BF16), k_ref[0, :, cols], NT) + bias
        highest = jnp.max(s, axis=-1, keepdims=True)
        w = jnp.exp(s - highest)
        total = jnp.sum(w, axis=-1, keepdims=True)
        o = dot(w.astype(BF16), v_ref[0, :, cols], NN) / total
        outs.append(o.astype(BF16))
        sums.append(highest + jnp.log(total))
    o_ref[0] = jnp.concatenate(outs, axis=-1)
    lse_ref[0] = jnp.concatenate(sums, axis=-1)


def attention_forward(q, k, v, bias_row, block):
    count, rows, width = q.shape
    heads = width // HD
    steps = rows // block
    some = pl.BlockSpec((1, block, width), lambda b, i: (b, i, 0))
    whole = pl.BlockSpec((1, rows, width), lambda b, i: (b, 0, 0))
    return pl.pallas_call(
        functools.partial(forward_kernel, heads),
        grid=(count, steps),
        in_specs=[some, whole, whole, pl.BlockSpec((1, 1, rows), lambda b, i: (b, 0, 0))],
        out_specs=[some, pl.BlockSpec((1, block, heads), lambda b, i: (b, i, 0))],
        out_shape=[
            jax.ShapeDtypeStruct((count, rows, width), BF16),
            jax.ShapeDtypeStruct((count, rows, heads), F32),
        ],
        compiler_params=pltpu.CompilerParams(vmem_limit_bytes=48 << 20),
        cost_estimate=pl.CostEstimate(
            flops=4 * count * rows * rows * width,
            bytes_accessed=8 * count * rows * width,
            transcendentals=count * heads * rows * rows,
        ),
    )(q, k, v, bias_row)


def backward_kernel(
    heads, q_ref, k_ref, v_ref, bias_ref, lse_ref, delta_ref, do_ref,
    dq_ref, dk_ref, dv_ref, dk_sum, dv_sum,
):
    step = pl.program_id(1)

    @pl.when(step == 0)
    def _():
        dk_sum[...] = jnp.zeros_like(dk_sum)
        dv_sum[...] = jnp.zeros_like(dv_sum)

    bias = bias_ref[0]
    dqs, dks, dvs = [], [], []
    for h in range(heads):
        cols = slice(h * HD, (h + 1) * HD)
        q = q_ref[0, :, cols] * jnp.asarray(0.125, BF16)
        k = k_ref[0, :, cols]
        do = do_ref[0, :, cols]
        s = dot(k, q, NT) + bias
        p = jnp.exp(s - lse_ref[0, 0, h : h + 1, :])
        dp = dot(v_ref[0, :, cols], do, NT)
        ds = (p * (dp - delta_ref[0, 0, h : h + 1, :])).astype(BF16)
        dqs.append(dot(ds, k, TN) * 0.125)
        dks.append(dot(ds, q, NN))
        dvs.append(dot(p.astype(BF16), do, NN))
    dq_ref[0] = jnp.concatenate(dqs, axis=-1).astype(BF16)
    dk_sum[...] += jnp.concatenate(dks, axis=-1)
    dv_sum[...] += jnp.concatenate(dvs, axis=-1)

    @pl.when(step == pl.num_programs(1) - 1)
    def _():
        dk_ref[0] = dk_sum[...].astype(BF16)
        dv_ref[0] = dv_sum[...].astype(BF16)


def attention_backward(q, k, v, bias_column, lse, delta, do, block):
    count, rows, width = q.shape
    heads = width // HD
    steps = rows // block
    some = pl.BlockSpec((1, block, width), lambda b, i: (b, i, 0))
    whole = pl.BlockSpec((1, rows, width), lambda b, i: (b, 0, 0))
    lines = pl.BlockSpec((1, 1, heads, block), lambda b, i: (b, i, 0, 0))

    def as_lines(values):
        return values.reshape(count, steps, block, heads).transpose(0, 1, 3, 2)

    shape = jax.ShapeDtypeStruct((count, rows, width), BF16)
    return pl.pallas_call(
        functools.partial(backward_kernel, heads),
        grid=(count, steps),
        in_specs=[
            some, whole, whole, pl.BlockSpec((1, rows, 1), lambda b, i: (b, 0, 0)),
            lines, lines, some,
        ],
        out_specs=[some, whole, whole],
        out_shape=[shape, shape, shape],
        scratch_shapes=[pltpu.VMEM((rows, width), F32), pltpu.VMEM((rows, width), F32)],
        compiler_params=pltpu.CompilerParams(vmem_limit_bytes=48 << 20),
        cost_estimate=pl.CostEstimate(
            flops=10 * count * rows * rows * width,
            bytes_accessed=14 * count * rows * width,
            transcendentals=count * heads * rows * rows,
        ),
    )(q, k, v, bias_column, as_lines(lse), as_lines(delta), do)


def forward_layer(section_in, hidden_keys, weight_set):
    w_qkv, w_proj, w_fc1, w_fc2, gains, biases, fc1_bias = weight_set
    seq_count = lax.axis_size("seq")
    group_width = D // seq_count
    image_count, local_rows = section_in.shape[:2]
    full_rows = local_rows * seq_count
    frames = section_in.astype(F32)
    normed_one, factor_one = layer_norm(frames)
    normed_in = (normed_one * gains[0] + biases[0]).astype(BF16)
    projected = jnp.einsum("bnd,de->bne", normed_in, w_qkv, preferred_element_type=F32)
    bias_row = jnp.concatenate([biases[1], jnp.zeros_like(biases[1]), biases[2]])
    packed = (projected + bias_row).astype(BF16)
    spread = lax.all_to_all(
        packed.reshape(image_count, local_rows, 3, seq_count, group_width),
        "seq",
        split_axis=3,
        concat_axis=1,
        tiled=True,
    ).reshape(image_count, full_rows, 3, group_width)
    head_sets = (spread[:, :, 0], spread[:, :, 1], spread[:, :, 2])
    merged, log_total = attention_forward(
        *head_sets, hidden_keys[:, None, :], local_rows
    )
    token_outs = lax.all_to_all(merged, "seq", split_axis=1, concat_axis=2, tiled=True)
    branch_one = jnp.einsum("bnd,de->bne", token_outs, w_proj, preferred_element_type=F32) + biases[3]
    residual = frames + gains[1] * branch_one
    normed_two, factor_two = layer_norm(residual)
    second = (normed_two * gains[2] + biases[4]).astype(BF16)
    hidden = jnp.einsum("bnd,df->bnf", second, w_fc1, preferred_element_type=F32) + fc1_bias
    active = gelu_value(hidden).astype(BF16)
    branch_two = jnp.einsum("bnf,fd->bnd", active, w_fc2, preferred_element_type=F32) + biases[5]
    output = (residual + gains[3] * branch_two).astype(BF16)
    kept = (
        normed_one, factor_one, normed_in, head_sets, merged, log_total, token_outs,
        branch_one, normed_two, factor_two, second, hidden, active, branch_two,
    )
    return (output, kept)


def backward_layer(kept, cotangent, hidden_keys, weight_set):
    w_qkv, w_proj, w_fc1, w_fc2, gains, biases, fc1_bias = weight_set
    (
        normed_one, factor_one, normed_in, head_sets, merged, log_total, token_outs,
        branch_one, normed_two, factor_two, second, hidden, active, branch_two,
    ) = kept
    seq_count = lax.axis_size("seq")
    group_width = D // seq_count
    image_count, local_rows = cotangent.shape[:2]
    full_rows = local_rows * seq_count
    token_axes = (0, 1)

    def total(values):
        return jnp.sum(values, axis=token_axes, dtype=F32)

    def weight_grad(left, right):
        whole = jnp.einsum("bnd,bne->de", left, right, preferred_element_type=F32)
        return lax.psum_scatter(whole.astype(BF16), ALL, scatter_dimension=0, tiled=True)

    upstream = cotangent.astype(F32)
    grad_branch = (gains[3] * upstream).astype(BF16)
    grad_scale_two = total(branch_two * upstream)
    grad_bias_out = total(grad_branch)
    grad_down = weight_grad(active, grad_branch)
    grad_active = jnp.einsum("bnd,fd->bnf", grad_branch, w_fc2, preferred_element_type=F32)
    grad_hidden = (grad_active * gelu_slope(hidden)).astype(BF16)
    grad_bias_mid = total(grad_hidden)
    grad_upper = weight_grad(second, grad_hidden)
    grad_second = jnp.einsum("bnf,df->bnd", grad_hidden, w_fc1, preferred_element_type=F32)
    grad_gain_two = total(grad_second * normed_two)
    grad_shift_two = total(grad_second)
    grad_resid = upstream + norm_back(grad_second * gains[2], normed_two, factor_two)
    grad_attend = (gains[1] * grad_resid).astype(BF16)
    grad_scale_one = total(branch_one * grad_resid)
    grad_bias_proj = total(grad_attend)
    grad_outproj = weight_grad(token_outs, grad_attend)
    grad_merged = jnp.einsum(
        "bne,de->bnd", grad_attend, w_proj, preferred_element_type=F32
    ).astype(BF16)
    head_upward = lax.all_to_all(
        grad_merged.reshape(image_count, local_rows, seq_count, group_width),
        "seq",
        split_axis=2,
        concat_axis=1,
        tiled=True,
    ).reshape(image_count, full_rows, group_width)
    delta = jnp.sum(
        (head_upward.astype(F32) * merged.astype(F32)).reshape(image_count, full_rows, -1, HD),
        axis=-1,
    )
    head_grads = attention_backward(
        *head_sets, hidden_keys[:, :, None], log_total, delta, head_upward, local_rows
    )
    grad_packed = lax.all_to_all(
        jnp.stack(head_grads, axis=2), "seq", split_axis=1, concat_axis=3, tiled=True
    ).reshape(image_count, local_rows, 3 * D)
    grad_inproj = weight_grad(normed_in, grad_packed)
    grad_bias_query = total(grad_packed[..., :D])
    grad_bias_value = total(grad_packed[..., 2 * D :])
    grad_entry = jnp.einsum("bne,de->bnd", grad_packed, w_qkv, preferred_element_type=F32)
    grad_gain_one = total(grad_entry * normed_one)
    grad_shift_one = total(grad_entry)
    grad_frames = grad_resid + norm_back(grad_entry * gains[0], normed_one, factor_one)
    rows = jnp.stack(
        [
            grad_gain_one, grad_scale_one, grad_gain_two, grad_scale_two,
            grad_shift_one, grad_bias_query, grad_bias_value, grad_bias_proj,
            grad_shift_two, grad_bias_out,
        ]
    )
    return (
        grad_frames.astype(BF16),
        (grad_inproj, grad_outproj, grad_upper, grad_down),
        (rows, grad_bias_mid),
    )


def per_device(images, key_mask, w_qkv, w_proj, w_fc1, w_fc2, gains, biases, fc1_bias, out_grad):
    core = lax.axis_index("pipe")
    low = core == 0
    dp_count = lax.axis_size("dp")
    shards = lax.axis_size("seq") * dp_count
    image_count = images.shape[0] // lax.axis_size("pipe")

    def my_images(array):
        return lax.dynamic_slice_in_dim(array, core * image_count, image_count, axis=0)

    part = gains.shape[2]
    small = jnp.concatenate([gains[0], biases[0], fc1_bias[0].reshape(-1, part)], axis=0)
    small = lax.all_gather(small, ("pipe", "dp"), axis=0)
    visible = lax.all_gather(my_images(key_mask), "seq", axis=1, tiled=True) > 0
    hidden_keys = jnp.where(visible, 0.0, -1e30).astype(F32)

    halves = []
    for tensor in (w_qkv[0], w_proj[0], w_fc1[0], w_fc2[0]):
        half = tensor.shape[0] // 2
        keep = lax.dynamic_slice_in_dim(tensor, core * half, half, axis=0)
        received = swap(lax.dynamic_slice_in_dim(tensor, (1 - core) * half, half, axis=0))
        halves.append((jnp.where(low, keep, received), jnp.where(low, received, keep)))

    sets = []
    for layer in range(2):
        rest = small[layer * dp_count : (layer + 1) * dp_count]
        lines = rest[:, :10].transpose(1, 0, 2).reshape(10, D)
        mids = rest[:, 10:].reshape(-1)
        whole = tuple(
            lax.all_gather(pair[layer], ("dp", "pipe"), axis=0, tiled=True) for pair in halves
        )
        sets.append((*whole, lines[:4], lines[4:], mids))

    middle, kept_zero = forward_layer(my_images(images), hidden_keys, sets[0])
    final, kept_one = forward_layer(middle, hidden_keys, sets[1])
    section_outputs = to_sections(middle, final, 0)[None]
    grad_middle, weights_one, vectors_one = backward_layer(
        kept_one, my_images(out_grad), hidden_keys, sets[1]
    )
    grad_first, weights_zero, vectors_zero = backward_layer(
        kept_zero, grad_middle, hidden_keys, sets[0]
    )
    input_grads = to_sections(grad_first, grad_middle, 0)[None]

    packed = []
    for rows, mids in (vectors_zero, vectors_one):
        lines = rows.reshape(10, shards, -1).transpose(1, 0, 2).reshape(shards, -1)
        packed.append(jnp.concatenate([lines, mids.reshape(shards, -1)], axis=1))
    mine = lax.psum_scatter(
        jnp.concatenate(packed, axis=0), ("pipe", "seq", "dp"), scatter_dimension=0, tiled=True
    )[0]
    width = D // shards
    lines = mine[: 10 * width].reshape(10, width)
    weights = [
        to_sections(zero, one, 0).astype(F32)[None]
        for zero, one in zip(weights_zero, weights_one)
    ]
    return (
        section_outputs,
        input_grads,
        *weights,
        lines[:4][None],
        lines[4:][None],
        mine[10 * width :][None],
    )


def solution(mesh):
    in_specs = (
        P("dp", "seq", None),
        P("dp", "seq"),
        P("pipe", "dp", None),
        P("pipe", "dp", None),
        P("pipe", "dp", None),
        P("pipe", "dp", None),
        P("pipe", None, "dp"),
        P("pipe", None, "dp"),
        P("pipe", "dp"),
        P("dp", "seq", None),
    )
    out_specs = (
        P("pipe", "dp", "seq", None),
        P("pipe", "dp", "seq", None),
        P("pipe", ("seq", "dp"), None),
        P("pipe", ("seq", "dp"), None),
        P("pipe", ("seq", "dp"), None),
        P("pipe", ("seq", "dp"), None),
        P("pipe", None, ("seq", "dp")),
        P("pipe", None, ("seq", "dp")),
        P("pipe", ("seq", "dp")),
    )
    return jax.shard_map(
        per_device, mesh=mesh, in_specs=in_specs, out_specs=out_specs, check_vma=False
    )
```

```python
import functools

import jax
import jax.numpy as jnp
from jax import lax
from jax.experimental import pallas as pl
from jax.experimental.pallas import tpu as pltpu
from jax.sharding import PartitionSpec as P

D = 1024
H = 16
HD = 64

epsilon = 1e-06
root_half = 0.7071067811865476
inv_root_tau = 0.3989422804014327
SHARDS = ("seq", "dp")
F32 = jnp.float32
BF16 = jnp.bfloat16


def layer_norm(values):
    centre = jnp.mean(values, axis=-1, keepdims=True)
    shifted = values - centre
    factor = lax.rsqrt(jnp.mean(shifted * shifted, axis=-1, keepdims=True) + epsilon)
    return (shifted * factor, factor)


def norm_back(upward, normed, factor):
    inner = (
        upward
        - jnp.mean(upward, axis=-1, keepdims=True)
        - normed * jnp.mean(upward * normed, axis=-1, keepdims=True)
    )
    return factor * inner


def gelu_value(hidden):
    return 0.5 * hidden * (1.0 + lax.erf(hidden * root_half))


def gelu_slope(hidden):
    return (
        0.5 * (1.0 + lax.erf(hidden * root_half))
        + hidden * jnp.exp(-0.5 * hidden * hidden) * inv_root_tau
    )


def swap(block):
    return lax.ppermute(block, "pipe", [(0, 1), (1, 0)])


def to_sections(first, second, axis):
    low = lax.axis_index("pipe") == 0
    mine = jnp.where(low, first, second)
    theirs = swap(jnp.where(low, second, first))
    return jnp.where(
        low,
        jnp.concatenate([mine, theirs], axis=axis),
        jnp.concatenate([theirs, mine], axis=axis),
    )


NT = (((1,), (1,)), ((), ()))
NN = (((1,), (0,)), ((), ()))
TN = (((0,), (0,)), ((), ()))


def dot(a, b, dims):
    return lax.dot_general(a, b, dims, preferred_element_type=F32)


def forward_kernel(heads, q_ref, k_ref, v_ref, bias_ref, o_ref, lse_ref):
    bias = bias_ref[0]
    outs, sums = [], []
    for h in range(heads):
        cols = slice(h * HD, (h + 1) * HD)
        s = dot(q_ref[0, :, cols] * jnp.asarray(0.125, BF16), k_ref[0, :, cols], NT) + bias
        highest = jnp.max(s, axis=-1, keepdims=True)
        w = jnp.exp(s - highest)
        total = jnp.sum(w, axis=-1, keepdims=True)
        o = dot(w.astype(BF16), v_ref[0, :, cols], NN) / total
        outs.append(o.astype(BF16))
        sums.append(highest + jnp.log(total))
    o_ref[0] = jnp.concatenate(outs, axis=-1)
    lse_ref[0] = jnp.concatenate(sums, axis=-1)


def attention_forward(q, k, v, bias_row, block):
    count, rows, width = q.shape
    heads = width // HD
    steps = rows // block
    some = pl.BlockSpec((1, block, width), lambda b, i: (b, i, 0))
    whole = pl.BlockSpec((1, rows, width), lambda b, i: (b, 0, 0))
    return pl.pallas_call(
        functools.partial(forward_kernel, heads),
        grid=(count, steps),
        in_specs=[some, whole, whole, pl.BlockSpec((1, 1, rows), lambda b, i: (b, 0, 0))],
        out_specs=[some, pl.BlockSpec((1, block, heads), lambda b, i: (b, i, 0))],
        out_shape=[
            jax.ShapeDtypeStruct((count, rows, width), BF16),
            jax.ShapeDtypeStruct((count, rows, heads), F32),
        ],
        compiler_params=pltpu.CompilerParams(vmem_limit_bytes=48 << 20),
        cost_estimate=pl.CostEstimate(
            flops=4 * count * rows * rows * width,
            bytes_accessed=8 * count * rows * width,
            transcendentals=count * heads * rows * rows,
        ),
    )(q, k, v, bias_row)


def backward_kernel(
    heads, q_ref, k_ref, v_ref, bias_ref, lse_ref, delta_ref, do_ref,
    dq_ref, dk_ref, dv_ref, dk_sum, dv_sum,
):
    step = pl.program_id(1)

    @pl.when(step == 0)
    def _():
        dk_sum[...] = jnp.zeros_like(dk_sum)
        dv_sum[...] = jnp.zeros_like(dv_sum)

    bias = bias_ref[0]
    dqs, dks, dvs = [], [], []
    for h in range(heads):
        cols = slice(h * HD, (h + 1) * HD)
        q = q_ref[0, :, cols] * jnp.asarray(0.125, BF16)
        k = k_ref[0, :, cols]
        do = do_ref[0, :, cols]
        s = dot(k, q, NT) + bias
        p = jnp.exp(s - lse_ref[0, 0, h : h + 1, :])
        dp = dot(v_ref[0, :, cols], do, NT)
        ds = (p * (dp - delta_ref[0, 0, h : h + 1, :])).astype(BF16)
        dqs.append(dot(ds, k, TN) * 0.125)
        dks.append(dot(ds, q, NN))
        dvs.append(dot(p.astype(BF16), do, NN))
    dq_ref[0] = jnp.concatenate(dqs, axis=-1).astype(BF16)
    dk_sum[...] += jnp.concatenate(dks, axis=-1)
    dv_sum[...] += jnp.concatenate(dvs, axis=-1)

    @pl.when(step == pl.num_programs(1) - 1)
    def _():
        dk_ref[0] = dk_sum[...].astype(BF16)
        dv_ref[0] = dv_sum[...].astype(BF16)


def attention_backward(q, k, v, bias_column, lse, delta, do, block):
    count, rows, width = q.shape
    heads = width // HD
    steps = rows // block
    some = pl.BlockSpec((1, block, width), lambda b, i: (b, i, 0))
    whole = pl.BlockSpec((1, rows, width), lambda b, i: (b, 0, 0))
    lines = pl.BlockSpec((1, 1, heads, block), lambda b, i: (b, i, 0, 0))

    def as_lines(values):
        return values.reshape(count, steps, block, heads).transpose(0, 1, 3, 2)

    shape = jax.ShapeDtypeStruct((count, rows, width), BF16)
    return pl.pallas_call(
        functools.partial(backward_kernel, heads),
        grid=(count, steps),
        in_specs=[
            some, whole, whole, pl.BlockSpec((1, rows, 1), lambda b, i: (b, 0, 0)),
            lines, lines, some,
        ],
        out_specs=[some, whole, whole],
        out_shape=[shape, shape, shape],
        scratch_shapes=[pltpu.VMEM((rows, width), F32), pltpu.VMEM((rows, width), F32)],
        compiler_params=pltpu.CompilerParams(vmem_limit_bytes=48 << 20),
        cost_estimate=pl.CostEstimate(
            flops=10 * count * rows * rows * width,
            bytes_accessed=14 * count * rows * width,
            transcendentals=count * heads * rows * rows,
        ),
    )(q, k, v, bias_column, as_lines(lse), as_lines(delta), do)


def forward_layer(section_in, hidden_keys, weight_set):
    w_qkv, w_proj, w_fc1, w_fc2, gains, biases, fc1_bias = weight_set
    seq_count = lax.axis_size("seq")
    group_width = D // seq_count
    image_count, local_rows = section_in.shape[:2]
    full_rows = local_rows * seq_count
    frames = section_in.astype(F32)
    normed_one, factor_one = layer_norm(frames)
    normed_in = (normed_one * gains[0] + biases[0]).astype(BF16)
    projected = jnp.einsum("bnd,de->bne", normed_in, w_qkv, preferred_element_type=F32)
    bias_row = jnp.concatenate([biases[1], jnp.zeros_like(biases[1]), biases[2]])
    packed = (projected + bias_row).astype(BF16)
    spread = lax.all_to_all(
        packed.reshape(image_count, local_rows, 3, seq_count, group_width),
        "seq",
        split_axis=3,
        concat_axis=1,
        tiled=True,
    ).reshape(image_count, full_rows, 3, group_width)
    head_sets = (spread[:, :, 0], spread[:, :, 1], spread[:, :, 2])
    merged, log_total = attention_forward(
        *head_sets, hidden_keys[:, None, :], local_rows
    )
    token_outs = lax.all_to_all(merged, "seq", split_axis=1, concat_axis=2, tiled=True)
    branch_one = jnp.einsum("bnd,de->bne", token_outs, w_proj, preferred_element_type=F32) + biases[3]
    residual = frames + gains[1] * branch_one
    normed_two, factor_two = layer_norm(residual)
    second = (normed_two * gains[2] + biases[4]).astype(BF16)
    hidden = jnp.einsum("bnd,df->bnf", second, w_fc1, preferred_element_type=F32) + fc1_bias
    active = gelu_value(hidden).astype(BF16)
    branch_two = jnp.einsum("bnf,fd->bnd", active, w_fc2, preferred_element_type=F32) + biases[5]
    output = (residual + gains[3] * branch_two).astype(BF16)
    kept = (
        normed_one, factor_one, normed_in, head_sets, merged, log_total, token_outs,
        branch_one, normed_two, factor_two, second, hidden, active, branch_two,
    )
    return (output, kept)


def backward_layer(kept, cotangent, hidden_keys, weight_set, early, late):
    w_qkv, w_proj, w_fc1, w_fc2, gains, biases, fc1_bias = weight_set
    (
        normed_one, factor_one, normed_in, head_sets, merged, log_total, token_outs,
        branch_one, normed_two, factor_two, second, hidden, active, branch_two,
    ) = kept
    core = lax.axis_index("pipe")
    seq_count = lax.axis_size("seq")
    group_width = D // seq_count
    image_count, local_rows = cotangent.shape[:2]
    full_rows = local_rows * seq_count
    token_axes = (0, 1)

    def total(values):
        return jnp.sum(values, axis=token_axes, dtype=F32)

    def weight_grad(left, right):
        whole = jnp.einsum("bnd,bne->de", left, right, preferred_element_type=F32).astype(BF16)
        half = whole.shape[1] // 2
        mine = lax.dynamic_slice_in_dim(whole, core * half, half, axis=1)
        theirs = swap(lax.dynamic_slice_in_dim(whole, (1 - core) * half, half, axis=1))
        both = (mine.astype(F32) + theirs.astype(F32)).astype(BF16)
        return lax.psum_scatter(both, SHARDS, scatter_dimension=0, tiled=True)

    upstream = cotangent.astype(F32)
    grad_branch = (gains[3] * upstream).astype(BF16)
    grad_scale_two = total(branch_two * upstream)
    grad_bias_out = total(grad_branch)
    grad_down = weight_grad(active, grad_branch)
    grad_active = jnp.einsum("bnd,fd->bnf", grad_branch, w_fc2, preferred_element_type=F32)
    grad_hidden = (grad_active * gelu_slope(hidden)).astype(BF16)
    grad_bias_mid = total(grad_hidden)
    grad_upper = weight_grad(second, grad_hidden)
    grad_second = jnp.einsum("bnf,df->bnd", grad_hidden, w_fc1, preferred_element_type=F32)
    grad_gain_two = total(grad_second * normed_two)
    grad_shift_two = total(grad_second)
    grad_resid = upstream + norm_back(grad_second * gains[2], normed_two, factor_two)
    grad_attend = (gains[1] * grad_resid).astype(BF16)
    grad_scale_one = total(branch_one * grad_resid)
    grad_bias_proj = total(grad_attend)
    grad_outproj = weight_grad(token_outs, grad_attend)
    grad_merged = jnp.einsum(
        "bne,de->bnd", grad_attend, w_proj, preferred_element_type=F32
    ).astype(BF16)
    head_upward = lax.all_to_all(
        grad_merged.reshape(image_count, local_rows, seq_count, group_width),
        "seq",
        split_axis=2,
        concat_axis=1,
        tiled=True,
    ).reshape(image_count, full_rows, group_width)
    head_upward, early = lax.optimization_barrier((head_upward, early))
    delta = jnp.sum(
        (head_upward.astype(F32) * merged.astype(F32)).reshape(image_count, full_rows, -1, HD),
        axis=-1,
    )
    head_grads = attention_backward(
        *head_sets, hidden_keys[:, :, None], log_total, delta, head_upward, local_rows
    )
    grad_packed = lax.all_to_all(
        jnp.stack(head_grads, axis=2), "seq", split_axis=1, concat_axis=3, tiled=True
    ).reshape(image_count, local_rows, 3 * D)
    grad_packed, grad_down, late = lax.optimization_barrier((grad_packed, grad_down, late))
    grad_inproj = weight_grad(normed_in, grad_packed)
    grad_bias_query = total(grad_packed[..., :D])
    grad_bias_value = total(grad_packed[..., 2 * D :])
    grad_entry = jnp.einsum("bne,de->bnd", grad_packed, w_qkv, preferred_element_type=F32)
    grad_gain_one = total(grad_entry * normed_one)
    grad_shift_one = total(grad_entry)
    grad_frames = grad_resid + norm_back(grad_entry * gains[0], normed_one, factor_one)
    rows = jnp.stack(
        [
            grad_gain_one, grad_scale_one, grad_gain_two, grad_scale_two,
            grad_shift_one, grad_bias_query, grad_bias_value, grad_bias_proj,
            grad_shift_two, grad_bias_out,
        ]
    )
    return (
        grad_frames.astype(BF16),
        (grad_inproj, grad_outproj, grad_upper, grad_down),
        (rows, grad_bias_mid),
        early,
        late,
    )


def per_device(images, key_mask, w_qkv, w_proj, w_fc1, w_fc2, gains, biases, fc1_bias, out_grad):
    core = lax.axis_index("pipe")
    low = core == 0
    dp_count = lax.axis_size("dp")
    shards = lax.axis_size("seq") * dp_count
    image_count = images.shape[0] // lax.axis_size("pipe")

    def my_images(array):
        return lax.dynamic_slice_in_dim(array, core * image_count, image_count, axis=0)

    part = gains.shape[2]
    small = jnp.concatenate([gains[0], biases[0], fc1_bias[0].reshape(-1, part)], axis=0)
    small = lax.all_gather(small, ("pipe", "dp"), axis=0)
    visible = my_images(lax.all_gather(key_mask, "seq", axis=1, tiled=True)) > 0
    hidden_keys = jnp.where(visible, 0.0, -1e30).astype(F32)

    halves = []
    for tensor in (w_qkv[0], w_proj[0], w_fc1[0], w_fc2[0]):
        half = tensor.shape[0] // 2
        keep = lax.dynamic_slice_in_dim(tensor, core * half, half, axis=0)
        received = swap(lax.dynamic_slice_in_dim(tensor, (1 - core) * half, half, axis=0))
        halves.append((jnp.where(low, keep, received), jnp.where(low, received, keep)))

    sets = []
    for layer in range(2):
        rest = small[layer * dp_count : (layer + 1) * dp_count]
        lines = rest[:, :10].transpose(1, 0, 2).reshape(10, D)
        mids = rest[:, 10:].reshape(-1)
        whole = tuple(
            lax.all_gather(pair[layer], ("dp", "pipe"), axis=0, tiled=True) for pair in halves
        )
        sets.append((*whole, lines[:4], lines[4:], mids))

    middle, kept_zero = forward_layer(my_images(images), hidden_keys, sets[0])
    final, kept_one = forward_layer(middle, hidden_keys, sets[1])
    section_outputs = to_sections(middle, final, 0)[None]
    grad_middle, weights_one, vectors_one, _, _ = backward_layer(
        kept_one, my_images(out_grad), hidden_keys, sets[1], (), ()
    )
    inproj_one, outproj_one, upper_one, down_one = weights_one
    grad_first, weights_zero, vectors_zero, (upper_one,), (inproj_one, outproj_one) = backward_layer(
        kept_zero, grad_middle, hidden_keys, sets[0], (upper_one,), (inproj_one, outproj_one)
    )
    weights_one = (inproj_one, outproj_one, upper_one, down_one)
    input_grads = to_sections(grad_first, grad_middle, 0)[None]

    packed = []
    for rows, mids in (vectors_zero, vectors_one):
        lines = rows.reshape(10, shards, -1).transpose(1, 0, 2).reshape(shards, -1)
        packed.append(jnp.concatenate([lines, mids.reshape(shards, -1)], axis=1))
    both = jnp.where(low, packed[0], packed[1]) + swap(jnp.where(low, packed[1], packed[0]))
    mine = lax.psum_scatter(
        both.reshape(shards * 8, -1), SHARDS, scatter_dimension=0, tiled=True
    ).reshape(-1)
    width = D // shards
    lines = mine[: 10 * width].reshape(10, width)
    weights = [
        to_sections(zero, one, 1).astype(F32)[None]
        for zero, one in zip(weights_zero, weights_one)
    ]
    return (
        section_outputs,
        input_grads,
        *weights,
        lines[:4][None],
        lines[4:][None],
        mine[10 * width :][None],
    )


def solution(mesh):
    in_specs = (
        P("dp", "seq", None),
        P("dp", "seq"),
        P("pipe", "dp", None),
        P("pipe", "dp", None),
        P("pipe", "dp", None),
        P("pipe", "dp", None),
        P("pipe", None, "dp"),
        P("pipe", None, "dp"),
        P("pipe", "dp"),
        P("dp", "seq", None),
    )
    out_specs = (
        P("pipe", "dp", "seq", None),
        P("pipe", "dp", "seq", None),
        P("pipe", ("seq", "dp"), None),
        P("pipe", ("seq", "dp"), None),
        P("pipe", ("seq", "dp"), None),
        P("pipe", ("seq", "dp"), None),
        P("pipe", None, ("seq", "dp")),
        P("pipe", None, ("seq", "dp")),
        P("pipe", ("seq", "dp")),
    )
    return jax.shard_map(
        per_device, mesh=mesh, in_specs=in_specs, out_specs=out_specs, check_vma=False
    )
```
